32 devices in a mesh: gx: 4 (over x, core), gy: 8 (over z, y).
Axes of the slice: x: 2, y: 2, z: 4, core: 2. Of those that a mesh axis runs over, the one named last changes fastest.
Arguments:
- activation: bfloat16 [32, 4096, 4096], P(None, 'gx', 'gy'), may hold values from -6 to 6
- cotangent: bfloat16 [32, 4096, 4096], P(None, 'gx', 'gy'), may hold values from -6 to 6
- point_weight: bfloat16 [32, 32], replicated, may hold values from -1 to 1
- spectral_weight: bfloat16 [2, 32, 32, 4096], P(None, None, None, ('gx', 'gy')), may hold values from -12 to 12
Outputs:
- grad_activation: bfloat16 [32, 4096, 4096], P(None, 'gx', 'gy')
- grad_point: float32 [32, 32], replicated
- grad_spectral: float32 [2, 32, 32, 4096], P(None, None, None, ('gx', 'gy'))
The draws below stay inside these ranges and needn't reach their ends.
All inputs are finite; a program needn't handle non-finite values.
Results may differ from the reference program's by a relative error of at most 0.0065.
Values sent between devices are 32-bit elements; how exact they have to be, the bound alone decides.
A program may use at most 384 MiB of HBM per device.

```python
import math
import jax
import jax.numpy as jnp
from jax import lax

CHANNELS = 32
GRID_X = 4096
GRID_Y = 4096
MODES_X = 64
MODES_Y = 64
MODES = 4096


def level_of(stream_key, dims, pieces, least, high):
    level, own = 1.0, jax.random.fold_in(stream_key, 6)
    for position, shards_of in pieces:
        draws = jnp.exp(jax.random.uniform(jax.random.fold_in(own, position), (shards_of,), jnp.float32, least / len(pieces), high / len(pieces)))
        level = level * jnp.repeat(draws, dims[position] // shards_of).reshape([-1 if axis == position else 1 for axis in range(len(dims))])
    return level


def gaussian(own_key, extent, deviation, most, split=(), kind=jnp.bfloat16):
    drawn = jax.random.normal(own_key, extent, jnp.float32) * deviation
    if len(split) > 0:
        drawn = level_of(own_key, extent, split, -0.22, 0.18) * drawn
    return jnp.clip(drawn, min=-most, max=most).astype(kind)


def setup_inputs(seed: int = 0) -> dict:
    arg_keys = jax.random.split(jax.random.key(seed), 5)
    return {
        "activation": gaussian(arg_keys[0], (CHANNELS, GRID_X, GRID_Y), 1.0, 6.0, ((1, 4), (2, 8))),
        "cotangent": gaussian(arg_keys[1], (CHANNELS, GRID_X, GRID_Y), 1.0, 6.0, ((1, 4), (2, 8))),
        "point_weight": gaussian(arg_keys[2], (CHANNELS, CHANNELS), CHANNELS ** -0.5, 1.0),
        "spectral_weight": gaussian(arg_keys[3], (2, CHANNELS, CHANNELS, MODES), 2.0, 12.0, ((3, 32),)),
    }


def spectrum_of(values):
    norm_scale = 1.0 / math.sqrt(GRID_X * GRID_Y)
    half_modes = MODES_X // 2

    def per_channel(channel_plane):
        along = jnp.fft.rfft(channel_plane.astype(jnp.float32), axis=1)[:, :MODES_Y]
        along = jnp.fft.fft(along, axis=0)
        kept = jnp.concatenate([along[:half_modes], along[GRID_X - half_modes:]], axis=0)
        return jnp.stack([jnp.real(kept), jnp.imag(kept)]).reshape(2, MODES_X * MODES_Y)
    stacked = lax.map(per_channel, values)
    return jnp.transpose(stacked, (1, 0, 2)) * norm_scale

def field_of(spectrum):
    norm_scale = 1.0 / math.sqrt(GRID_X * GRID_Y)
    half_modes = MODES_X // 2

    def per_channel(mode_pair):
        complex_modes = lax.complex(mode_pair[0], mode_pair[1]).reshape(MODES_X, MODES_Y)
        gap_rows = jnp.zeros((GRID_X - MODES_X, MODES_Y), complex_modes.dtype)
        padded = jnp.concatenate([complex_modes[:half_modes], gap_rows, complex_modes[half_modes:]], axis=0)
        columns = jnp.fft.ifft(padded, axis=0) * GRID_X
        gap_cols = jnp.zeros((GRID_X, GRID_Y - MODES_Y), columns.dtype)
        full_grid = jnp.concatenate([columns, gap_cols], axis=1)
        return jnp.real(jnp.fft.ifft(full_grid, axis=1)) * (GRID_Y * norm_scale)
    return lax.map(per_channel, jnp.transpose(spectrum, (1, 0, 2)))

def mix_modes(weight, spectrum):
    real_part = jnp.einsum('ocm,cm->om', weight[0], spectrum[0]) - jnp.einsum('ocm,cm->om', weight[1], spectrum[1])
    imag_part = jnp.einsum('ocm,cm->om', weight[0], spectrum[1]) + jnp.einsum('ocm,cm->om', weight[1], spectrum[0])
    return jnp.stack([real_part, imag_part])

def mix_adjoint(weight, spectrum):
    real_part = jnp.einsum('ocm,om->cm', weight[0], spectrum[0]) + jnp.einsum('ocm,om->cm', weight[1], spectrum[1])
    imag_part = jnp.einsum('ocm,om->cm', weight[0], spectrum[1]) - jnp.einsum('ocm,om->cm', weight[1], spectrum[0])
    return jnp.stack([real_part, imag_part])

def gelu_slope(values):
    cumulative = 0.5 * (1.0 + jax.scipy.special.erf(values * 0.7071067811865476))
    return cumulative + values * jnp.exp(-0.5 * values * values) * 0.3989422804014327

def reference(activation, cotangent, point_weight, spectral_weight):
    norm_scale = 1.0 / math.sqrt(GRID_X * GRID_Y)
    weight_full = spectral_weight.astype(jnp.float32)
    point_full = point_weight.astype(jnp.float32)
    forward_modes = spectrum_of(activation)
    spectral_part = field_of(mix_modes(weight_full, forward_modes))
    block_rows = min(GRID_X, 256)
    block_count = GRID_X // block_rows
    block_ids = jnp.arange(block_count, dtype=jnp.int32)

    def forward_block(running, block_index):
        hidden_all, grad_sum = running
        row_start = (block_index * block_rows).astype(jnp.int32)
        act_block = lax.dynamic_slice_in_dim(activation, row_start, block_rows, 1).astype(jnp.float32)
        spec_block = lax.dynamic_slice_in_dim(spectral_part, row_start, block_rows, 1)
        cot_block = lax.dynamic_slice_in_dim(cotangent, row_start, block_rows, 1).astype(jnp.float32)
        pre_block = jnp.einsum('oc,cxy->oxy', point_full, act_block) + spec_block
        hidden_block = (cot_block * gelu_slope(pre_block)).astype(jnp.bfloat16)
        hidden_all = lax.dynamic_update_slice_in_dim(hidden_all, hidden_block, row_start, 1)
        grad_sum = grad_sum + jnp.einsum('oxy,cxy->oc', hidden_block.astype(jnp.float32), act_block)
        return ((hidden_all, grad_sum), None)
    start_state = (jnp.zeros(activation.shape, jnp.bfloat16), jnp.zeros((CHANNELS, CHANNELS), jnp.float32))
    (hidden, grad_sum), unused = lax.scan(forward_block, start_state, block_ids)
    grad_point = grad_sum * norm_scale
    back_modes = spectrum_of(hidden)
    grad_real = back_modes[0][:, None, :] * forward_modes[0][None, :, :] + back_modes[1][:, None, :] * forward_modes[1][None, :, :]
    grad_imag = back_modes[1][:, None, :] * forward_modes[0][None, :, :] - back_modes[0][:, None, :] * forward_modes[1][None, :, :]
    grad_spectral = jnp.stack([grad_real, grad_imag])
    back_field = field_of(mix_adjoint(weight_full, back_modes))

    def backward_block(grad_all, block_index):
        row_start = (block_index * block_rows).astype(jnp.int32)
        hidden_block = lax.dynamic_slice_in_dim(hidden, row_start, block_rows, 1).astype(jnp.float32)
        back_block = lax.dynamic_slice_in_dim(back_field, row_start, block_rows, 1)
        grad_block = (jnp.einsum('oc,oxy->cxy', point_full, hidden_block) + back_block).astype(jnp.bfloat16)
        return (lax.dynamic_update_slice_in_dim(grad_all, grad_block, row_start, 1), None)
    grad_activation, unused = lax.scan(backward_block, jnp.zeros(activation.shape, jnp.bfloat16), block_ids)
    return (grad_activation, grad_point, grad_spectral)
```

```python
import functools
import math

import jax
import jax.numpy as jnp
from jax import lax
from jax.experimental import pallas as pl
from jax.experimental.pallas import tpu as pltpu
from jax.sharding import PartitionSpec as P

GRID_X = 4096
GRID_Y = 4096
MODES_X = 64
MODES_Y = 64


def twiddles(rows_here, cols_here):
    two_pi = 2.0 * math.pi
    row_start = lax.axis_index("gx") * rows_here
    col_start = lax.axis_index("gy") * cols_here
    freq_y = jnp.arange(MODES_Y, dtype=jnp.int32)
    col_ids = col_start + jnp.arange(cols_here, dtype=jnp.int32)
    phase_y = (col_ids[:, None] * freq_y[None, :] % GRID_Y).astype(jnp.float32) * (two_pi / GRID_Y)
    raw_x = jnp.arange(MODES_X, dtype=jnp.int32)
    freq_x = jnp.where(raw_x < MODES_X // 2, raw_x, raw_x + GRID_X - MODES_X)
    row_ids = row_start + jnp.arange(rows_here, dtype=jnp.int32)
    phase_x = (freq_x[:, None] * row_ids[None, :] % GRID_X).astype(jnp.float32) * (two_pi / GRID_X)
    return (jnp.cos(phase_y), jnp.sin(phase_y), jnp.cos(phase_x), jnp.sin(phase_x))


def mix_modes(weight, spectrum):
    real_part = jnp.einsum("ocm,cm->om", weight[0], spectrum[0]) - jnp.einsum(
        "ocm,cm->om", weight[1], spectrum[1]
    )
    imag_part = jnp.einsum("ocm,cm->om", weight[0], spectrum[1]) + jnp.einsum(
        "ocm,cm->om", weight[1], spectrum[0]
    )
    return jnp.stack([real_part, imag_part])


def mix_adjoint(weight, spectrum):
    real_part = jnp.einsum("ocm,om->cm", weight[0], spectrum[0]) + jnp.einsum(
        "ocm,om->cm", weight[1], spectrum[1]
    )
    imag_part = jnp.einsum("ocm,om->cm", weight[0], spectrum[1]) - jnp.einsum(
        "ocm,om->cm", weight[1], spectrum[0]
    )
    return jnp.stack([real_part, imag_part])


def gelu_slope(values):
    cumulative = 0.5 * (1.0 + jax.scipy.special.erf(values * 0.7071067811865476))
    return cumulative + values * jnp.exp(-0.5 * values * values) * 0.3989422804014327


SUB = 16


def split(table):
    high = table.astype(jnp.bfloat16)
    return high, (table - high.astype(jnp.float32)).astype(jnp.bfloat16)


def forward_kernel(values_ref, table_y_ref, table_x_ref, out_ref):
    both = jnp.dot(values_ref[0], table_y_ref[...], preferred_element_type=jnp.float32)
    width = 2 * MODES_Y
    along = both[:, :width] + both[:, width:]
    high = along.astype(jnp.bfloat16)
    low = (along - high.astype(jnp.float32)).astype(jnp.bfloat16)
    joined = jnp.concatenate([high, low], axis=1)
    parts = jnp.dot(table_x_ref[...], joined, preferred_element_type=jnp.float32)
    parts = parts[:, :width] + parts[:, width:]
    parts = parts[: 2 * MODES_X] + parts[2 * MODES_X :]
    upper = parts[:MODES_X]
    lower = pltpu.roll(parts[MODES_X:], MODES_Y, 1)
    lane = lax.broadcasted_iota(jnp.int32, upper.shape, 1)
    out_ref[0] = jnp.where(lane < MODES_Y, upper - lower, -(upper + lower))


def forward_local(values, table_y, table_x):
    channels, rows, cols = values.shape
    norm_scale = 1.0 / math.sqrt(GRID_X * GRID_Y)
    out = pl.pallas_call(
        forward_kernel,
        grid=(channels,),
        out_shape=jax.ShapeDtypeStruct((channels, MODES_X, 2 * MODES_Y), jnp.float32),
        in_specs=[
            pl.BlockSpec((1, rows, cols), lambda c: (c, 0, 0)),
            pl.BlockSpec(table_y.shape, lambda c: (0, 0)),
            pl.BlockSpec(table_x.shape, lambda c: (0, 0)),
        ],
        out_specs=pl.BlockSpec((1, MODES_X, 2 * MODES_Y), lambda c: (c, 0, 0)),
        name="forward_modes",
    )(values, table_y, table_x)
    out = out.reshape(channels, MODES_X, 2, MODES_Y).transpose(2, 0, 1, 3) * norm_scale
    return out.reshape(2 * channels, MODES_X * MODES_Y)


def rows_kernel(modes_ref, table_ref, out_ref):
    modes = modes_ref[0].astype(jnp.bfloat16)
    value = jnp.dot(
        table_ref[...], jnp.concatenate([modes, modes], axis=0), preferred_element_type=jnp.float32
    )
    out_ref[0] = value.astype(jnp.bfloat16)


def rows_of(spectrum, table):
    channels = spectrum.shape[1]
    norm_scale = 1.0 / math.sqrt(GRID_X * GRID_Y)
    real = spectrum[0].reshape(channels, MODES_X, MODES_Y) * norm_scale
    imag = spectrum[1].reshape(channels, MODES_X, MODES_Y) * norm_scale
    modes = jnp.concatenate(
        [jnp.concatenate([real, imag], axis=2), jnp.concatenate([-imag, real], axis=2)], axis=1
    )
    rows = table.shape[0]
    return pl.pallas_call(
        rows_kernel,
        grid=(channels,),
        out_shape=jax.ShapeDtypeStruct((channels, rows, 2 * MODES_Y), jnp.bfloat16),
        in_specs=[
            pl.BlockSpec((1, 2 * MODES_X, 2 * MODES_Y), lambda c: (c, 0, 0)),
            pl.BlockSpec(table.shape, lambda c: (0, 0)),
        ],
        out_specs=pl.BlockSpec((1, rows, 2 * MODES_Y), lambda c: (c, 0, 0)),
        name="synthesis_rows",
    )(modes, table)


def field_block(mix_ref, flat, rows_ref, table_ref):
    rows = rows_ref[...].reshape(flat.shape[0], 2 * MODES_Y)
    value = jnp.dot(mix_ref[...], flat, preferred_element_type=jnp.float32)
    return value + jnp.dot(
        jnp.concatenate([rows, rows], axis=1), table_ref[...], preferred_element_type=jnp.float32
    )


def hidden_kernel(act_ref, cot_ref, rows_ref, mix_ref, table_ref, hidden_ref, point_ref, total):
    step = pl.program_id(0)
    channels, sub, cols = act_ref.shape
    size = channels * sub

    @pl.when(step == 0)
    def _():
        total[...] = jnp.zeros_like(total)

    flat = act_ref[...].reshape(size, cols)
    pre = field_block(mix_ref, flat, rows_ref, table_ref)
    slope = gelu_slope(pre)
    cot = cot_ref[...].reshape(size, cols).astype(jnp.float32)
    hidden = (cot * slope).astype(jnp.bfloat16)
    hidden_ref[...] = hidden.reshape(channels, sub, cols)
    total[...] += lax.dot_general(
        hidden, flat, (((1,), (1,)), ((), ())), preferred_element_type=jnp.float32
    )

    @pl.when(step == pl.num_programs(0) - 1)
    def _():
        row = lax.broadcasted_iota(jnp.int32, (size, size), 0)
        col = lax.broadcasted_iota(jnp.int32, (size, size), 1)
        kept = jnp.where(row % sub == col % sub, total[...], 0.0)
        pick_row = lax.broadcasted_iota(jnp.int32, (channels, size), 0)
        pick_col = lax.broadcasted_iota(jnp.int32, (channels, size), 1)
        pick = jnp.where(pick_col // sub == pick_row, 1.0, 0.0)
        half = jnp.dot(
            pick, kept, precision=lax.Precision.HIGHEST, preferred_element_type=jnp.float32
        )
        point_ref[...] = lax.dot_general(
            half,
            pick,
            (((1,), (1,)), ((), ())),
            precision=lax.Precision.HIGHEST,
            preferred_element_type=jnp.float32,
        )


def grad_kernel(hidden_ref, rows_ref, mix_ref, table_ref, out_ref):
    channels, sub, cols = hidden_ref.shape
    flat = hidden_ref[...].reshape(channels * sub, cols)
    value = field_block(mix_ref, flat, rows_ref, table_ref)
    out_ref[...] = value.astype(jnp.bfloat16).reshape(channels, sub, cols)


def block_of(width):
    return lambda channels: pl.BlockSpec((channels, SUB, width), lambda i: (0, i, 0))


def whole(array):
    return pl.BlockSpec(array.shape, lambda i: (0, 0))


def hidden_of(activation, cotangent, rows, mix, table):
    channels, rows_here, cols = activation.shape
    wide = block_of(cols)(channels)
    size = channels * SUB
    return pl.pallas_call(
        hidden_kernel,
        grid=(rows_here // SUB,),
        out_shape=(
            jax.ShapeDtypeStruct(activation.shape, jnp.bfloat16),
            jax.ShapeDtypeStruct((channels, channels), jnp.float32),
        ),
        in_specs=[wide, wide, block_of(2 * MODES_Y)(channels), whole(mix), whole(table)],
        out_specs=(wide, pl.BlockSpec((channels, channels), lambda i: (0, 0))),
        scratch_shapes=[pltpu.VMEM((size, size), jnp.float32)],
        name="hidden",
    )(activation, cotangent, rows, mix, table)


def grad_of(hidden, rows, mix, table):
    channels, rows_here, cols = hidden.shape
    wide = block_of(cols)(channels)
    return pl.pallas_call(
        grad_kernel,
        grid=(rows_here // SUB,),
        out_shape=jax.ShapeDtypeStruct(hidden.shape, jnp.bfloat16),
        in_specs=[wide, block_of(2 * MODES_Y)(channels), whole(mix), whole(table)],
        out_specs=wide,
        name="grad",
    )(hidden, rows, mix, table)


def own_sums(partial_value, devices):
    lines, modes = partial_value.shape
    chunks = partial_value.reshape(lines, devices, modes // devices).transpose(1, 0, 2)
    moved = lax.all_to_all(chunks, ("gx", "gy"), split_axis=0, concat_axis=0, tiled=True)
    return jnp.sum(moved, axis=0)


def spread(share):
    return lax.all_gather(share, ("gx", "gy"), axis=1, tiled=True)


def per_device(devices, activation, cotangent, point_weight, spectral_weight):
    channels, rows_here, cols_here = activation.shape
    norm_scale = 1.0 / math.sqrt(GRID_X * GRID_Y)
    cos_y, sin_y, cos_x, sin_x = twiddles(rows_here, cols_here)
    fwd_y = jnp.concatenate(split(jnp.concatenate([cos_y, sin_y], axis=1)), axis=1)
    fwd_x = jnp.concatenate(split(jnp.concatenate([cos_x, sin_x], axis=0)), axis=0)
    inv_x = jnp.concatenate(split(jnp.concatenate([cos_x.T, sin_x.T], axis=1)), axis=1)
    inv_y = jnp.concatenate(split(jnp.concatenate([cos_y.T, -sin_y.T], axis=0)), axis=0)
    eye = jnp.eye(SUB, dtype=jnp.bfloat16)
    mix_point = jnp.kron(point_weight, eye)
    mix_back = jnp.kron(point_weight.T, eye)
    weight_full = spectral_weight.astype(jnp.float32)
    mode_count = MODES_X * MODES_Y
    share = mode_count // devices

    forward_modes = own_sums(forward_local(activation, fwd_y, fwd_x), devices)
    forward_modes = forward_modes.reshape(2, channels, share)
    mixed = mix_modes(weight_full, forward_modes).reshape(2 * channels, share)
    rows = rows_of(spread(mixed).reshape(2, channels, mode_count), inv_x)
    hidden, local_grad = hidden_of(activation, cotangent, rows, mix_point, inv_y)

    back_partial = forward_local(hidden, fwd_y, fwd_x)
    each = channels * channels // devices
    point_lines = jnp.pad(local_grad.reshape(devices, each), ((0, 0), (0, share - each)))
    sums = own_sums(
        jnp.concatenate([back_partial, point_lines.reshape(1, mode_count)], axis=0), devices
    )
    back_modes = sums[: 2 * channels].reshape(2, channels, share)
    grad_real = (
        back_modes[0][:, None, :] * forward_modes[0][None, :, :]
        + back_modes[1][:, None, :] * forward_modes[1][None, :, :]
    )
    grad_imag = (
        back_modes[1][:, None, :] * forward_modes[0][None, :, :]
        - back_modes[0][:, None, :] * forward_modes[1][None, :, :]
    )
    grad_spectral = jnp.stack([grad_real, grad_imag])
    adjoint = mix_adjoint(weight_full, back_modes).reshape(2 * channels, share)
    gathered = spread(jnp.concatenate([adjoint, sums[2 * channels :]], axis=0))
    grad_point = gathered[2 * channels].reshape(devices, share)[:, :each]
    grad_point = grad_point.reshape(channels, channels) * norm_scale
    back_rows = rows_of(gathered[: 2 * channels].reshape(2, channels, mode_count), inv_x)
    grad_activation = grad_of(hidden, back_rows, mix_back, inv_y)
    return (grad_activation, grad_point, grad_spectral)


def solution(mesh):
    placed = (P(None, "gx", "gy"), P(None, "gx", "gy"), P(), P(None, None, None, ("gx", "gy")))
    return jax.shard_map(
        functools.partial(per_device, mesh.shape["gx"] * mesh.shape["gy"]),
        mesh=mesh,
        in_specs=placed,
        out_specs=(P(None, "gx", "gy"), P(), P(None, None, None, ("gx", "gy"))),
        check_vma=False,
    )
```
